32 devices in a mesh: groups: 2 (over y), seq: 4 (over z), tp: 4 (over x, core).
Axes of the slice: x: 2, y: 2, z: 4, core: 2. Of those that a mesh axis runs over, the one named last changes fastest.
Arguments:
- branches: bfloat16 [1024, 3, 2048], P(('groups', 'seq'), None, 'tp'), parts along dimension 0, may hold values from -5 to 5
- residual: bfloat16 [1024, 4096], P(('groups', 'seq'), 'tp'), parts along dimension 0, may hold values from -32 to 32
- segments: int32 [1024], P('groups'), parts along dimension 0, may hold values from 0 to 7, never falling along the last dimension, each value on 1 to 256 neighbouring positions
- long_filter: float32 [512, 2048], P('seq', 'tp'), may hold values from -4 to 4
- short_taps: float32 [3, 3, 2048], P(None, None, 'tp'), may hold values from -3 to 3
- skip_gain: float32 [2048], P('tp'), may hold values from -3 to 3
- out_weight: bfloat16 [2048, 4096], P(None, 'tp'), may hold values from -0.125 to 0.125
- norm_gain: float32 [4096], replicated, may hold values from 0.1 to 1.9
- head_weight: bfloat16 [4096, 3, 2048], P(None, None, 'tp'), may hold values from -27 to 27
Outputs:
- hidden: bfloat16 [1024, 4096], P(('groups', 'seq'), 'tp'), parts along dimension 0
- context: bfloat16 [1024, 2048], P(('groups', 'seq'), 'tp'), parts along dimension 0
The draws below stay inside these ranges and needn't reach their ends.
There are 2 independent parts, one for each index of `groups`. The reference program is written for one: setup_inputs(seed, part) draws one part's arguments, and reference() takes and returns one part's arrays. A program takes and returns all parts, laid end to end along the dimension named above; an argument that names none is the same for every part. Nothing has to cross between parts.
Inputs may be any that keep to these rules, and one draw needn't show every extreme that they name: `segments`: document ids never fall along the window; a document holds 1 to 256 positions, and one holds exactly 256.
All inputs are finite; a program needn't handle non-finite values.
Results may differ from the reference program's by a relative error of at most 0.017.
Values may be sent and summed in bfloat16 or wider, within the bound.
No kernel may reach another device: no remote copies, remote signals or barrier semaphores. Data moves between devices by JAX's collectives and lax.ppermute only.
A program may use at most 64 MiB of HBM per device.

```python
import math
import jax
import jax.numpy as jnp
import numpy as np
from jax import lax

D = 4096
C = 2048
H = 16
DH = 128
S_DEV = 128
L = 512


def draw_residual(key, part):
    keys = jax.random.split(jax.random.fold_in(key, 11), 3)
    rows = jnp.exp(jax.random.uniform(keys[0], (L, 1), minval=math.log(0.4), maxval=math.log(2.0)))
    rising = 3.0 ** (jnp.arange(D, dtype=jnp.float32) / D)
    spread = jnp.exp(jax.random.uniform(keys[1], (1, D), minval=math.log(0.5), maxval=math.log(2.0)))
    noise = jnp.clip(jax.random.normal(keys[2], (L, D)), -4.0, 4.0)
    values = noise * rows * rising[None, :] * spread / 1.5
    return values.astype(jnp.bfloat16)


def draw_long_filter(key, part):
    keys = jax.random.split(jax.random.fold_in(key, 23), 6)
    share = 0.5
    fast_life = jnp.exp(jax.random.uniform(keys[0], (C,), minval=math.log(S_DEV / 8.0), maxval=math.log(L / 2.0)))
    slow_life = jnp.exp(jax.random.uniform(keys[1], (C,), minval=math.log(2.0 * L), maxval=math.log(8.0 * L)))
    is_slow = jax.random.uniform(keys[2], (C,)) < share
    life = jnp.where(is_slow, slow_life, fast_life)
    time_steps = jnp.arange(L, dtype=jnp.float32)[:, None]
    decay_envelope = jnp.exp(-time_steps / life[None, :])
    spike_locations = jax.random.randint(keys[3], (2, C), 1, L)
    dropped_entries = jax.random.uniform(keys[4], (2, C), minval=0.5, maxval=0.8)
    for spike_signal in range(2):
        decay_envelope = decay_envelope * jnp.where(time_steps >= spike_locations[spike_signal][None, :].astype(jnp.float32), dropped_entries[spike_signal][None, :], 1.0)
    rough = jnp.clip(jax.random.normal(keys[5], (L, C)), -4.0, 4.0)
    norm = jnp.sqrt(jnp.sum(decay_envelope * decay_envelope, axis=0, keepdims=True))
    return (decay_envelope * rough / norm).astype(jnp.float32)


def draw_head_weight(key, part):
    keys = jax.random.split(jax.random.fold_in(key, 37), 1)
    weight = jnp.clip(jax.random.normal(keys[0], (D, 3, H * DH)), -4.0, 4.0) / math.sqrt(D)
    return weight.astype(jnp.bfloat16)


def shard_levels(own_key, dims, cuts, low, high):
    def one(axis_at, blocks):
        heights = jax.random.uniform(jax.random.fold_in(jax.random.fold_in(own_key, 6), axis_at), (blocks,), jnp.float32, low / len(cuts), high / len(cuts))
        return jnp.repeat(jnp.exp(heights), dims[axis_at] // blocks).reshape((-1,) + (1,) * (len(dims) - axis_at - 1))

    level = one(*cuts[0])
    for cut in cuts[1:]:
        level = level * one(*cut)
    return level


def profile(count, total, most, lean):
    loads = [(1 << 20) // math.isqrt(grade ** lean) + 1 for grade in range(2, count + 1)]
    spare, counts = total - most - (count - 1), [1] * (count - 1)
    while spare > 0:
        free = [i for i in range(count - 1) if counts[i] < most]
        whole, budget = sum([loads[i] for i in free]), spare
        for i in free:
            addition = min(most - counts[i], max(1, budget * loads[i] // whole), spare)
            counts[i] = counts[i] + addition
            spare = spare - addition
    return np.array([most] + counts)


def ragged_sizes(rng, number_of, total, reach, skew):
    if number_of == 2:
        one = jax.random.randint(rng, (), max(1, total - reach), min(reach, total - 1) + 1)
        return jnp.stack([one, total - one])
    sizes = jnp.asarray(profile(number_of, total, reach, skew), jnp.int32)
    couples = (number_of - 1) // 2
    source_of, taker = sizes[1:1 + 2 * couples:2], sizes[2:2 + 2 * couples:2]
    room = jnp.minimum(source_of - 1, reach - taker)
    shifted = jax.random.randint(jax.random.fold_in(rng, 1), (couples,), 0, 1 << 20) % (room + 1)
    sizes = sizes.at[1:1 + 2 * couples:2].set(source_of - shifted).at[2:2 + 2 * couples:2].set(taker + shifted)
    return sizes[jax.random.permutation(jax.random.fold_in(rng, 2), number_of)]


def scatter_about(stream_key, dims, width, most, shards=(), held_as=jnp.bfloat16):
    entries = jax.random.normal(stream_key, dims, jnp.float32) * width
    if len(shards) > 0:
        entries = shard_levels(stream_key, dims, shards, -0.22, 0.18) * entries
    return jnp.clip(entries, min=-most, max=most).astype(held_as)


def setup_inputs(seed: int = 0, part: int = 0) -> dict:
    seeds = jax.random.split(jax.random.key(seed), 10)
    part_splits = jax.random.split(jax.random.fold_in(seeds[9], part), 10)
    return {
        "branches": scatter_about(part_splits[0], (L, 3, C), 1.0, 5.0, ((0, 4), (2, 4))),
        "residual": draw_residual(jax.random.fold_in(jax.random.fold_in(seeds[9], part), 71), part),
        "segments": jnp.searchsorted(jnp.cumsum(ragged_sizes(part_splits[2], 8, L, L // 2, 0)), jnp.arange(L), side="right").astype(jnp.int32),
        "long_filter": draw_long_filter(jax.random.fold_in(seeds[9], 71), part),
        "short_taps": scatter_about(seeds[4], (3, 3, C), 0.6, 3.0, ((2, 4),), jnp.float32),
        "skip_gain": scatter_about(seeds[5], (C,), 1.0, 3.0, ((0, 4),), jnp.float32),
        "out_weight": scatter_about(seeds[6], (C, D), C ** -0.5, 0.125, ((1, 4),)),
        "norm_gain": jnp.clip(1.0 + 0.18 * jax.random.normal(seeds[7], (D,), jnp.float32), 0.1, 1.9),
        "head_weight": draw_head_weight(jax.random.fold_in(seeds[9], 71), part),
    }


EPSILON = 1e-05

def featurize(branches, short_taps, segments):
    values = branches.astype(jnp.float32)
    flagged_positions = jnp.concatenate([jnp.full((2,), -1, jnp.int32), segments.astype(jnp.int32)])
    padded = jnp.concatenate([jnp.zeros((2, 3, C), jnp.float32), values], axis=0)
    featured = jnp.zeros((L, 3, C), jnp.float32)
    for offset in range(3):
        earlier = padded[2 - offset:2 - offset + L]
        same = flagged_positions[2 - offset:2 - offset + L] == segments
        featured = featured + jnp.where(same[:, None, None], short_taps[:, offset, :][None] * earlier, 0.0)
    return featured

def reference(branches, residual, segments, long_filter, short_taps, skip_gain, out_weight, norm_gain, head_weight):
    featured = featurize(branches, short_taps, segments)
    mixed = featured[:, 1] * featured[:, 2]
    spectrum = jnp.fft.rfft(mixed, n=2 * L, axis=0) * jnp.fft.rfft(long_filter, n=2 * L, axis=0)
    conv = jnp.fft.irfft(spectrum, n=2 * L, axis=0)[:L]
    gated = (featured[:, 0] * (conv + skip_gain * mixed)).astype(jnp.bfloat16)
    mixed_out = jnp.dot(gated, out_weight, preferred_element_type=jnp.float32)
    hidden = (residual.astype(jnp.float32) + mixed_out).astype(jnp.bfloat16)
    wide = hidden.astype(jnp.float32)
    scale = lax.rsqrt(lax.optimization_barrier(jnp.mean(wide * wide, axis=1)) + EPSILON)
    normed = (wide * scale[:, None] * norm_gain).astype(jnp.bfloat16)
    projected = jnp.dot(normed, head_weight.reshape(D, 3 * H * DH), preferred_element_type=jnp.float32).astype(jnp.bfloat16)
    projected = projected.reshape(L, 3, H, DH).transpose(1, 2, 0, 3)
    positions = jnp.arange(L, dtype=jnp.int32)
    allowed = (positions[None, :] <= positions[:, None]) & (segments[None, :] == segments[:, None])
    factor = 1.0 / math.sqrt(DH)

    def one_head(operands):
        query, keys, values = operands
        score = jnp.dot(query, keys.T, preferred_element_type=jnp.float32) * factor
        peak = lax.optimization_barrier(jnp.max(jnp.where(allowed, score, -1e+30), axis=1, keepdims=True))
        weight = jnp.where(allowed, jnp.exp(score - peak), 0.0)
        mass = lax.optimization_barrier(jnp.sum(weight, axis=1, keepdims=True))
        total = jnp.dot(weight.astype(jnp.bfloat16), values, preferred_element_type=jnp.float32)
        return total / mass
    context = lax.map(one_head, (projected[0], projected[1], projected[2]))
    context = context.transpose(1, 0, 2).reshape(L, H * DH).astype(jnp.bfloat16)
    return (hidden, context)
```

```python
import functools
import math

import jax
import jax.numpy as jnp
import numpy as np
from jax import lax
from jax.experimental import pallas as pl
from jax.experimental.pallas import tpu as pltpu
from jax.sharding import PartitionSpec as P

DH = 128


EPSILON = 1e-05
HIGHEST = lax.Precision.HIGHEST
TWO_PI = 2.0 * math.pi


def passed_along(array, axis, by):
    count = lax.axis_size(axis)
    pairs = [(i, i + by) for i in range(count) if 0 <= i + by < count]
    return lax.ppermute(array, axis, pairs)


def complex_times(left_real, left_imag, right_real, right_imag):
    return (
        left_real * right_real - left_imag * right_imag,
        left_real * right_imag + left_imag * right_real,
    )


def window_convolve(whole, shards):
    count = whole.shape[1]
    rows = count // shards
    span = 2 * shards
    total = 2 * count
    data = whole.reshape(2, shards, rows, whole.shape[2])
    outer_index = jnp.arange(span, dtype=jnp.int32)
    block_index = jnp.arange(shards, dtype=jnp.int32)
    place_index = jnp.arange(rows, dtype=jnp.int32)
    outer = TWO_PI * (outer_index[:, None] * block_index[None, :] % span).astype(jnp.float32) / span
    outer_cos = jnp.cos(outer)
    outer_sin = jnp.sin(outer)
    first_real = jnp.einsum("ka,sabc->skbc", outer_cos, data, precision=HIGHEST)
    first_imag = -jnp.einsum("ka,sabc->skbc", outer_sin, data, precision=HIGHEST)
    twist = (
        TWO_PI * (outer_index[:, None] * place_index[None, :] % total).astype(jnp.float32) / total
    )
    twist_cos = jnp.cos(twist)[:, :, None]
    twist_sin = jnp.sin(twist)[:, :, None]
    turned_real, turned_imag = complex_times(first_real, first_imag, twist_cos, -twist_sin)
    inner = TWO_PI * (place_index[:, None] * place_index[None, :] % rows).astype(jnp.float32) / rows
    inner_cos = jnp.cos(inner)
    inner_sin = jnp.sin(inner)
    spec_real = jnp.einsum("bq,skbc->skqc", inner_cos, turned_real, precision=HIGHEST) + jnp.einsum(
        "bq,skbc->skqc", inner_sin, turned_imag, precision=HIGHEST
    )
    spec_imag = jnp.einsum("bq,skbc->skqc", inner_cos, turned_imag, precision=HIGHEST) - jnp.einsum(
        "bq,skbc->skqc", inner_sin, turned_real, precision=HIGHEST
    )
    prod_real, prod_imag = complex_times(spec_real[0], spec_imag[0], spec_real[1], spec_imag[1])
    back_real = jnp.einsum("qb,kqc->kbc", inner_cos, prod_real, precision=HIGHEST) - jnp.einsum(
        "qb,kqc->kbc", inner_sin, prod_imag, precision=HIGHEST
    )
    back_imag = jnp.einsum("qb,kqc->kbc", inner_cos, prod_imag, precision=HIGHEST) + jnp.einsum(
        "qb,kqc->kbc", inner_sin, prod_real, precision=HIGHEST
    )
    reverted_real, reverted_imag = complex_times(back_real, back_imag, twist_cos, twist_sin)
    result = jnp.einsum("ka,kbc->abc", outer_cos, reverted_real, precision=HIGHEST) - jnp.einsum(
        "ka,kbc->abc", outer_sin, reverted_imag, precision=HIGHEST
    )
    return (result / total).reshape(count, whole.shape[2])


def local(
    branches,
    residual,
    segments,
    long_filter,
    short_taps,
    skip_gain,
    out_weight,
    norm_gain,
    head_weight,
):
    rows = branches.shape[0]
    channels = branches.shape[2]
    shards = lax.axis_size("seq")
    rank = lax.axis_index("seq")
    first = rank * rows
    prior = passed_along(branches[rows - 2 :], "seq", 1)
    padded = jnp.concatenate([prior, branches], axis=0).astype(jnp.float32)
    flagged_positions = jnp.concatenate([jnp.full((2,), -1, jnp.int32), segments])
    window = lax.dynamic_slice_in_dim(flagged_positions, first, rows + 2)
    own_ids = window[2:]
    featured = jnp.zeros((rows, 3, channels), jnp.float32)
    for offset in range(3):
        earlier = padded[2 - offset : 2 - offset + rows]
        same = window[2 - offset : 2 - offset + rows] == own_ids
        featured = featured + jnp.where(
            same[:, None, None], short_taps[:, offset, :][None] * earlier, 0.0
        )
    mixed = featured[:, 1] * featured[:, 2]
    signals = jnp.stack([mixed, long_filter])
    whole = lax.all_to_all(signals, "seq", split_axis=2, concat_axis=1, tiled=True)
    columns = window_convolve(whole, shards)
    conv = lax.all_to_all(columns, "seq", split_axis=0, concat_axis=1, tiled=True)
    gated = (featured[:, 0] * (conv + skip_gain * mixed)).astype(jnp.bfloat16)
    weight_rows = out_weight
    mixed_out = jnp.dot(
        lax.all_gather(gated, "tp", axis=1, tiled=True),
        weight_rows,
        preferred_element_type=jnp.float32,
    )
    hidden = (residual.astype(jnp.float32) + mixed_out).astype(jnp.bfloat16)
    width = head_weight.shape[0]
    flat_weight = head_weight.reshape(width, -1)
    local_wide = hidden.astype(jnp.float32)
    squares = jnp.sum(local_wide * local_wide, axis=1)
    total_squares = lax.psum(squares, "tp")
    scale = lax.rsqrt(total_squares / width + EPSILON)
    local_width = hidden.shape[1]
    local_gain = lax.dynamic_slice_in_dim(
        norm_gain, lax.axis_index("tp") * local_width, local_width
    )
    normed = (local_wide * scale[:, None] * local_gain).astype(jnp.bfloat16)
    weight_rows = flat_weight
    projected = jnp.dot(
        lax.all_gather(normed, "tp", axis=1, tiled=True),
        weight_rows,
        preferred_element_type=jnp.float32,
    )
    projected = projected.astype(jnp.bfloat16).reshape(rows, 3, -1, DH)
    query = projected[:, 0]
    keys = projected[:, 1]
    values = projected[:, 2]
    local_heads = query.shape[1]
    factor = 1.0 / math.sqrt(DH)
    query_pos = first + jnp.arange(rows, dtype=jnp.int32)
    peak = jnp.full((rows, local_heads), -1e30, jnp.float32)
    piece_keys = lax.all_gather(keys, "seq", axis=0, tiled=True)
    piece_values = lax.all_gather(values, "seq", axis=0, tiled=True)
    count = piece_keys.shape[0]
    score = (
        jnp.einsum("qhd,khd->qhk", query, piece_keys, preferred_element_type=jnp.float32) * factor
    )
    key_pos = jnp.arange(count, dtype=jnp.int32)
    allowed = (key_pos[None, :] <= query_pos[:, None]) & (segments[None, :] == own_ids[:, None])
    allowed = allowed[:, None, :]
    masked_scores = jnp.where(allowed, score, -1e30)
    new_peak = jnp.maximum(peak, jnp.max(masked_scores, axis=2))
    weight = jnp.where(allowed, jnp.exp(score - new_peak[:, :, None]), 0.0)
    mass = jnp.sum(weight, axis=2)
    accum = jnp.einsum(
        "qhk,khd->qhd",
        weight.astype(jnp.bfloat16),
        piece_values,
        preferred_element_type=jnp.float32,
    )
    peak, mass, accum = (new_peak, mass, accum)
    context = (accum / mass[:, :, None]).reshape(rows, local_heads * DH).astype(jnp.bfloat16)
    return (hidden, context)


HEAD = 128
FLOOR = -1e30


def xor_exchange(array, axis, bit):
    count = lax.axis_size(axis)
    return lax.ppermute(array, axis, [(i, i ^ bit) for i in range(count)])


def rotated(array, axis):
    count = lax.axis_size(axis)
    return lax.ppermute(array, axis, [(i, (i + 1) % count) for i in range(count)])


def in_vmem():
    return pl.BlockSpec(memory_space=pltpu.VMEM)


def in_smem():
    return pl.BlockSpec(memory_space=pltpu.SMEM)


def call(kernel, outs, *operands, name, smem=1, scratch=(), flops=0, moved=0):
    specs = [in_smem()] * smem + [in_vmem()] * (len(operands) - smem)
    single = not isinstance(outs, (list, tuple))
    shapes = [outs] if single else list(outs)
    made = pl.pallas_call(
        kernel,
        out_shape=shapes,
        in_specs=specs,
        out_specs=[in_vmem()] * len(shapes),
        scratch_shapes=list(scratch),
        compiler_params=pltpu.CompilerParams(vmem_limit_bytes=16 << 20),
        cost_estimate=pl.CostEstimate(flops=flops, bytes_accessed=moved, transcendentals=0),
        name=name,
    )(*operands)
    return made[0] if single else made


def shape(dims, dtype):
    return jax.ShapeDtypeStruct(dims, dtype)


def fetched(weight, name):
    parts = 4
    step = weight.shape[0] // parts

    def kernel(source, target, sems):
        copies = [
            pltpu.make_async_copy(
                source.at[pl.ds(i * step, step)], target.at[pl.ds(i * step, step)], sems.at[i]
            )
            for i in range(parts)
        ]
        for copy in copies:
            copy.start()
        for copy in copies:
            copy.wait()

    return pl.pallas_call(
        kernel,
        out_shape=shape(weight.shape, weight.dtype),
        in_specs=[pl.BlockSpec(memory_space=pl.ANY)],
        out_specs=in_vmem(),
        scratch_shapes=[pltpu.SemaphoreType.DMA((parts,))],
        compiler_params=pltpu.CompilerParams(vmem_limit_bytes=1 << 20),
        cost_estimate=pl.CostEstimate(
            flops=0, bytes_accessed=2 * weight.size * weight.dtype.itemsize, transcendentals=0
        ),
        name=name,
    )(weight)


def dft_tables(count):
    total = 2 * count
    k = np.arange(count)[:, None]
    t = np.arange(count)[None, :]
    angle = 2.0 * np.pi * ((k * t) % total) / total
    real = np.cos(angle)
    imag = -np.sin(angle)
    imag[0] = np.where(np.arange(count) % 2 == 0, 1.0, -1.0)
    forward = np.concatenate([real, imag], axis=0)
    share = np.full((total, 1), 2.0 / total)
    share[0] = 1.0 / total
    share[count] = 1.0 / total
    backward = (forward * share).T
    return forward, backward


def pre_kernel(rank_ref, b_ref, h_ref, *piece_refs):
    n = len(piece_refs)
    rows, ch = h_ref.shape
    sub = ch // n
    tail = b_ref[0, rows - 16 : rows, :].astype(jnp.float32)[14:16]
    halo = jnp.concatenate([tail[:, c * sub : (c + 1) * sub] for c in range(n)], axis=0)
    halo = jnp.concatenate([halo, jnp.zeros((16 - 2 * n, sub), jnp.float32)], axis=0)
    for k in range(n):
        dest = rank_ref[0] ^ k
        lanes = pl.ds(pl.multiple_of(dest * sub, sub), sub)
        out = piece_refs[k]
        out[0:rows] = b_ref[1, :, lanes]
        out[rows : 2 * rows] = b_ref[2, :, lanes]
        out[2 * rows : 3 * rows] = h_ref[:, lanes].astype(jnp.bfloat16)
        out[3 * rows :] = halo.astype(jnp.bfloat16)


def filtered(padded_ref, taps, same, branch, count):
    total = taps[branch, 0:1, :] * padded_ref[8 : 8 + count, :]
    for back in (1, 2):
        term = taps[branch, back : back + 1, :] * padded_ref[8 - back : 8 - back + count, :]
        total = total + jnp.where(same[back], term, 0.0)
    return total


def conv_kernel(n, rank_ref, segs_ref, taps_ref, skip_ref, fwd_ref, bwd_ref, *refs):
    pieces, outs, (one, two, both) = refs[:n], refs[n : 2 * n], refs[2 * n :]
    sub = pieces[0].shape[1]
    count = segs_ref.shape[0]
    rows = count // n
    rank = rank_ref[0]
    one[0:8] = jnp.zeros((8, sub), jnp.float32)
    two[0:8] = jnp.zeros((8, sub), jnp.float32)
    for k in range(n):
        first = (rank ^ k) * rows
        here = pl.ds(pl.multiple_of(first + 8, 8), rows)
        one[here] = pieces[k][0:rows].astype(jnp.float32)
        two[here] = pieces[k][rows : 2 * rows].astype(jnp.float32)
        both[pl.ds(pl.multiple_of(first, rows), rows), sub:] = pieces[k][2 * rows : 3 * rows]
    lanes = pl.ds(pl.multiple_of(rank * sub, sub), sub)
    taps = taps_ref[:, :, lanes]
    own = segs_ref[:, 0:1]
    same = [None] + [segs_ref[:, back : back + 1] == own for back in (1, 2)]
    mixed = filtered(one, taps, same, 1, count) * filtered(two, taps, same, 2, count)
    both[:, 0:sub] = mixed.astype(jnp.bfloat16)
    spec = jnp.dot(fwd_ref[...], both[...], preferred_element_type=jnp.float32)
    xr, hr = spec[:count, :sub], spec[:count, sub:]
    xi, hi = spec[count:, :sub], spec[count:, sub:]
    edge = lax.broadcasted_iota(jnp.int32, (count, sub), 0) == 0
    rr, ii = xr * hr, xi * hi
    prod_r = jnp.where(edge, rr, rr - ii)
    prod_i = jnp.where(edge, ii, xr * hi + xi * hr)
    prod = jnp.concatenate([prod_r.astype(jnp.bfloat16), prod_i.astype(jnp.bfloat16)], axis=0)
    conv = jnp.dot(bwd_ref[...], prod, preferred_element_type=jnp.float32)
    conv = conv + skip_ref[:, lanes] * mixed
    one[pl.ds(8, count)] = conv
    for k in range(n):
        first = (rank ^ k) * rows
        outs[k][...] = one[pl.ds(pl.multiple_of(first + 8, 8), rows)].astype(jnp.bfloat16)


def outer_kernel(n, rank_ref, segs_ref, taps_ref, b_ref, *refs):
    pieces, out, pad = refs[: n - 1], refs[n - 1], refs[n]
    rows, ch = out.shape
    sub = ch // n
    rank = rank_ref[0]
    back = rank ^ jnp.maximum(rank - 1, 0)
    halo = jnp.zeros((16, sub), jnp.float32)
    for k in range(1, n):
        halo = jnp.where(back == k, pieces[k - 1][3 * rows :].astype(jnp.float32), halo)
    for c in range(n):
        pad[6:8, c * sub : (c + 1) * sub] = halo[2 * c : 2 * c + 2]
    pad[8 : 8 + rows] = b_ref[0].astype(jnp.float32)
    own = segs_ref[:, 0:1]
    same = [None] + [segs_ref[:, k : k + 1] == own for k in (1, 2)]
    out[...] = filtered(pad, taps_ref[...], same, 0, rows)


def gate_kernel(n, rank_ref, outer_ref, *refs):
    outs = refs[n]
    sub = refs[0].shape[1]
    for k in range(n):
        lanes = pl.ds(pl.multiple_of((rank_ref[0] ^ k) * sub, sub), sub)
        value = outer_ref[:, lanes] * refs[k][...].astype(jnp.float32)
        outs[:, lanes] = value.astype(jnp.bfloat16)


def block_dot(block, weight_ref, index):
    depth = block.shape[1]
    here = pl.ds(pl.multiple_of(index * depth, depth), depth)
    return jnp.dot(block, weight_ref[here, :], preferred_element_type=jnp.float32)


def out_first_kernel(tp_ref, own_ref, mate_ref, weight_ref, acc_ref):
    acc_ref[...] = block_dot(own_ref[...], weight_ref, tp_ref[0]) + block_dot(
        mate_ref[...], weight_ref, tp_ref[0] ^ 1
    )


def out_add_kernel(tp_ref, block_ref, weight_ref, acc_ref, res_ref, next_ref):
    next_ref[...] = (
        acc_ref[...]
        + res_ref[...].astype(jnp.float32)
        + block_dot(block_ref[...], weight_ref, tp_ref[0] ^ 2)
    )


def out_last_kernel(tp_ref, block_ref, weight_ref, acc_ref, hidden_ref):
    total = acc_ref[...] + block_dot(block_ref[...], weight_ref, tp_ref[0] ^ 3)
    hidden_ref[...] = total.astype(jnp.bfloat16)


def gained(block_ref, gain_ref, index):
    depth = block_ref.shape[1]
    wide = block_ref[...].astype(jnp.float32)
    here = pl.ds(pl.multiple_of(index * depth, depth), depth)
    squares = jnp.sum(wide * wide, axis=1, keepdims=True)
    return (wide * gain_ref[:, here]).astype(jnp.bfloat16), squares


def head_dots(block, weight_ref, index, kinds):
    depth = block.shape[1]
    here = pl.ds(pl.multiple_of(index * depth, depth), depth)
    return [
        jnp.dot(block, weight_ref[kind, here, :], preferred_element_type=jnp.float32)
        for kind in kinds
    ]


def head_first_kernel(tp_ref, own_ref, mate_ref, gain_ref, weight_ref, acc_ref, sq_ref):
    own, sq_own = gained(own_ref, gain_ref, tp_ref[0])
    mate, sq_mate = gained(mate_ref, gain_ref, tp_ref[0] ^ 1)
    for kind in range(3):
        acc_ref[kind] = (
            head_dots(own, weight_ref, tp_ref[0], (kind,))[0]
            + head_dots(mate, weight_ref, tp_ref[0] ^ 1, (kind,))[0]
        )
    sq_ref[...] = jnp.broadcast_to(sq_own + sq_mate, sq_ref.shape)


def head_add_kernel(tp_ref, block_ref, gain_ref, weight_ref, acc_ref, sq_ref, next_ref, nsq_ref):
    block, squares = gained(block_ref, gain_ref, tp_ref[0] ^ 2)
    for kind in range(3):
        next_ref[kind] = acc_ref[kind] + head_dots(block, weight_ref, tp_ref[0] ^ 2, (kind,))[0]
    nsq_ref[...] = sq_ref[...] + squares


def head_last_kernel(
    kind, width, tp_ref, block_ref, gain_ref, weight_ref, acc_ref, sq_ref, out_ref
):
    block, squares = gained(block_ref, gain_ref, tp_ref[0] ^ 3)
    scale = lax.rsqrt((sq_ref[:, 0:1] + squares) / width + EPSILON)
    total = acc_ref[kind] + head_dots(block, weight_ref, tp_ref[0] ^ 3, (kind,))[0]
    out_ref[...] = (total * scale).astype(jnp.bfloat16)


def attend_kernel(blocks, query_segs_ref, key_segs_ref, q_ref, *refs):
    keys, values, out = refs[:blocks], refs[blocks : 2 * blocks], refs[2 * blocks]
    rows = q_ref.shape[0]
    factor = 1.0 / math.sqrt(HEAD)
    own = query_segs_ref[:, 0:1]
    allowed = []
    for j in range(blocks):
        same = key_segs_ref[:, (blocks - 1 - j) * rows : (blocks - j) * rows] == own
        if j == 0:
            at = lax.broadcasted_iota(jnp.int32, (rows, rows), 0)
            past = lax.broadcasted_iota(jnp.int32, (rows, rows), 1)
            same = same & (past <= at)
        allowed.append(same)
    for h in range(q_ref.shape[1] // HEAD):
        lanes = slice(h * HEAD, (h + 1) * HEAD)
        query = q_ref[:, lanes]
        scores = []
        for j in range(blocks):
            score = lax.dot_general(
                query,
                keys[j][:, lanes],
                (((1,), (1,)), ((), ())),
                preferred_element_type=jnp.float32,
            )
            scores.append(jnp.where(allowed[j], score * factor, FLOOR))
        peak = scores[0]
        for score in scores[1:]:
            peak = jnp.maximum(peak, score)
        peak = jnp.max(peak, axis=1, keepdims=True)
        mass = jnp.zeros((rows, 1), jnp.float32)
        accum = jnp.zeros((rows, HEAD), jnp.float32)
        for j in range(blocks):
            weight = jnp.where(allowed[j], jnp.exp(scores[j] - peak), 0.0)
            mass = mass + jnp.sum(weight, axis=1, keepdims=True)
            accum = accum + jnp.dot(
                weight.astype(jnp.bfloat16),
                values[j][:, lanes],
                preferred_element_type=jnp.float32,
            )
        out[:, lanes] = (accum / mass).astype(jnp.bfloat16)


def fast_local(
    branches,
    residual,
    segments,
    long_filter,
    short_taps,
    skip_gain,
    out_weight,
    norm_gain,
    head_weight,
):
    rows, _, ch = branches.shape
    n = lax.axis_size("seq")
    count = segments.shape[0]
    sub = ch // n
    out_width = out_weight.shape[1]
    width = head_weight.shape[0]
    rank = lax.axis_index("seq").astype(jnp.int32)
    rank1 = rank.reshape(1)
    tp1 = lax.axis_index("tp").astype(jnp.int32).reshape(1)
    f32, bf16 = jnp.float32, jnp.bfloat16

    planes = branches.transpose(1, 0, 2)
    taps = short_taps.transpose(1, 0, 2) if False else short_taps
    gain = norm_gain.reshape(1, width)
    heads = head_weight.transpose(1, 0, 2)

    piece = shape((3 * rows + 16, sub), bf16)
    pieces = call(pre_kernel, [piece] * n, rank1, planes, long_filter, name="pre")
    came = {}
    for k in range(n - 1, 0, -1):
        with jax.named_scope(f"toowner{k}"):
            came[k] = xor_exchange(pieces[k], "seq", k)
    got = [pieces[0]] + [came[k] for k in range(1, n)]

    reach = -(-(count // 2 - 1) // rows)
    flagged = jnp.concatenate([jnp.full((reach * rows,), -1, jnp.int32), segments])
    near = lax.dynamic_slice_in_dim(flagged, rank * rows, (reach + 1) * rows)
    lead = reach * rows
    own_segs = jnp.stack([near[lead - k : lead - k + rows] for k in range(3)], axis=1)
    all_segs = jnp.stack([flagged[lead - k : lead - k + count] for k in range(3)], axis=1)

    w_out = fetched(out_weight, "fetchout")
    w_head = fetched(heads.reshape(3 * width, ch), "fetchhead").reshape(3, width, ch)

    forward, backward = dft_tables(count)
    back_piece = shape((rows, sub), bf16)
    conv = call(
        functools.partial(conv_kernel, n),
        [back_piece] * n,
        rank1,
        all_segs,
        taps,
        skip_gain.reshape(1, ch),
        jnp.asarray(forward, bf16),
        jnp.asarray(backward, bf16),
        *got,
        name="conv",
        scratch=[
            pltpu.VMEM((count + 8, sub), f32),
            pltpu.VMEM((count + 8, sub), f32),
            pltpu.VMEM((count, 2 * sub), bf16),
        ],
    )
    back = {}
    for k in range(n - 1, 0, -1):
        with jax.named_scope(f"fromowner{k}"):
            back[k] = xor_exchange(conv[k], "seq", k)
    outer = call(
        functools.partial(outer_kernel, n),
        shape((rows, ch), f32),
        rank1,
        own_segs,
        taps,
        planes,
        *got[1:],
        name="outer",
        scratch=[pltpu.VMEM((rows + 8, ch), f32)],
    )
    gated = call(
        functools.partial(gate_kernel, n),
        shape((rows, ch), bf16),
        rank1,
        outer,
        conv[0],
        *[back[k] for k in range(1, n)],
        name="gate",
    )

    with jax.named_scope("gfar"):
        far = xor_exchange(gated, "tp", 2)
    with jax.named_scope("gmate"):
        mate = xor_exchange(gated, "tp", 1)
    acc = call(out_first_kernel, shape((rows, out_width), f32), tp1, gated, mate, w_out, name="outa")
    with jax.named_scope("gfarmate"):
        far_mate = xor_exchange(far, "tp", 1)
    acc = call(
        out_add_kernel, shape((rows, out_width), f32), tp1, far, w_out, acc, residual, name="outb"
    )
    hidden = call(
        out_last_kernel, shape((rows, out_width), bf16), tp1, far_mate, w_out, acc, name="outc"
    )

    with jax.named_scope("hfar"):
        far = xor_exchange(hidden, "tp", 2)
    with jax.named_scope("hmate"):
        mate = xor_exchange(hidden, "tp", 1)
    acc_shape, sq_shape = shape((3, rows, ch), f32), shape((rows, 128), f32)
    acc, sq = call(
        head_first_kernel, [acc_shape, sq_shape], tp1, hidden, mate, gain, w_head, name="heada"
    )
    with jax.named_scope("hfarmate"):
        far_mate = xor_exchange(far, "tp", 1)
    acc, sq = call(
        head_add_kernel, [acc_shape, sq_shape], tp1, far, gain, w_head, acc, sq, name="headb"
    )
    made = {}
    for kind, name in ((1, "headk"), (2, "headv"), (0, "headq")):
        made[kind] = call(
            functools.partial(head_last_kernel, kind, width),
            shape((rows, ch), bf16),
            tp1,
            far_mate,
            gain,
            w_head,
            acc,
            sq,
            name=name,
        )
    keys, values = [made[1]], [made[2]]
    for step in range(reach):
        with jax.named_scope(f"key{step}"):
            keys.append(rotated(keys[-1], "seq"))
        with jax.named_scope(f"value{step}"):
            values.append(rotated(values[-1], "seq"))
    context = call(
        functools.partial(attend_kernel, reach + 1),
        shape((rows, ch), bf16),
        own_segs,
        near.reshape(1, -1),
        made[0],
        *keys,
        *values,
        smem=0,
        name="attend",
    )
    return hidden, context


def suits(mesh, args):
    branches, segments = args[0], args[2]
    n, tp = mesh.shape["seq"], mesh.shape["tp"]
    parts = mesh.shape["groups"]
    count = segments.shape[0] // parts
    sub = branches.shape[2] // (tp * n)
    return tp == 4 and n & (n - 1) == 0 and 2 * n <= 16 and sub % 128 == 0 and count <= 1024


def solution(mesh):
    placed = (
        P(("groups", "seq"), None, "tp"),
        P(("groups", "seq"), "tp"),
        P("groups"),
        P("seq", "tp"),
        P(None, None, "tp"),
        P("tp"),
        P(None, "tp"),
        P(),
        P(None, None, "tp"),
    )

    def whole(*args):
        return jax.shard_map(
            fast_local if suits(mesh, args) else local,
            mesh=mesh,
            in_specs=placed,
            out_specs=(P(("groups", "seq"), "tp"), P(("groups", "seq"), "tp")),
            check_vma=False,
        )(*args)

    return whole
```
